768 devices in a mesh: lat: 24 (over z_lo, x, core), lon: 32 (over y, z_hi).
Axes of the slice: x: 4, y: 8, z: 12 (z_hi: 4, z_lo: 3; z = z_hi * 3 + z_lo), core: 2. Of those that a mesh axis runs over, the one named last changes fastest.
Arguments:
- fields: bfloat16 [384, 512, 1024], P('lat', 'lon'), may hold values from -6 to 6
- gain_conv: float32 [1024], replicated, may hold values from 0.1 to 1.9
- w_depth: float32 [7, 7, 1024], replicated, may hold values from -0.875 to 0.875
- w_layer: bfloat16 [1024, 3072], P(None, 'lat'), as said below
- gain_attn: float32 [1024], replicated, may hold values from 0.1 to 1.9
- gain_out: float32 [1024], replicated, may hold values from 0.1 to 1.9
Outputs:
- layer_out: bfloat16 [384, 512, 1024], P('lat', 'lon')
The draws below stay inside these ranges and needn't reach their ends.
Inputs may be any that keep to these rules, and one draw needn't show every extreme that they name: `w_layer`: independent entries of mean zero; the scale of a column lies between 1 / sqrt(1024) and 20 / sqrt(1024), and no entry exceeds 80 / sqrt(1024) in magnitude.
All inputs are finite; a program needn't handle non-finite values.
Results may differ from the reference program's by a relative error of at most 0.012.
The reference program's roundings to bfloat16 on the way (of `normed`, `conv_out`, `attn_in`, `projected` and `probs`) count: a program that leaves them out, or rounds other values in their place, can miss the bound.
Values may be sent and summed in bfloat16 or wider, within the bound.
A program may use at most 32 MiB of HBM per device.

```python
import jax
import jax.numpy as jnp
from jax import lax

LAT_DEV = 16
LON_DEV = 16
C = 1024
HEAD_DIM = 64
KERNEL = 7
REACH = 3
H = 384
W = 512


def draw_w_layer(key, part):
    base = jax.random.truncated_normal(key, -4.0, 4.0, (C, 3 * C), jnp.float32) * C ** (-0.5)
    return base.astype(jnp.bfloat16)


def shard_levels(own_key, shape, shards, smallest, largest):
    def one(position, parts):
        steps = jax.random.uniform(jax.random.fold_in(jax.random.fold_in(own_key, 6), position), (parts,), jnp.float32, smallest / len(shards), largest / len(shards))
        return jnp.repeat(jnp.exp(steps), shape[position] // parts).reshape((-1,) + (1,) * (len(shape) - position - 1))

    factor_of = one(*shards[0])
    for cut in shards[1:]:
        factor_of = factor_of * one(*cut)
    return factor_of


def normal_values(rng, shape, deviation, limit, pieces=(), kind=jnp.bfloat16):
    loudness = shard_levels(rng, shape, pieces, -0.22, 0.18) if pieces else 1.0
    entries = jax.random.normal(rng, shape, jnp.float32) * deviation * loudness
    return jnp.minimum(jnp.maximum(entries, -limit), limit).astype(kind)


def setup_inputs(seed: int = 0) -> dict:
    seeds = jax.random.split(jax.random.key(seed), 7)
    return {
        "fields": normal_values(seeds[0], (H, W, C), 1.0, 6.0, ((0, 24), (1, 32))),
        "gain_conv": jnp.clip(1.0 + 0.18 * jax.random.normal(seeds[1], (C,), jnp.float32), 0.1, 1.9),
        "w_depth": normal_values(seeds[2], (KERNEL, KERNEL, C), (KERNEL * KERNEL) ** -0.5, 0.875, (), jnp.float32),
        "w_layer": draw_w_layer(jax.random.fold_in(seeds[6], 71), 0),
        "gain_attn": jnp.clip(1.0 + 0.18 * jax.random.normal(seeds[4], (C,), jnp.float32), 0.1, 1.9),
        "gain_out": jnp.clip(1.0 + 0.18 * jax.random.normal(seeds[5], (C,), jnp.float32), 0.1, 1.9),
    }


epsilon = 1e-06

def rms_scale(values, gain):
    return values * lax.rsqrt(lax.optimization_barrier(jnp.mean(values * values, axis=-1, keepdims=True)) + epsilon) * gain

def depthwise(padded, w_depth, lat_rows, lon_cols):
    total = jnp.zeros((lat_rows, lon_cols, padded.shape[2]), jnp.float32)
    for row_off in range(KERNEL):
        for col_off in range(KERNEL):
            window = padded[row_off:row_off + lat_rows, col_off:col_off + lon_cols].astype(jnp.float32)
            total = total + window * w_depth[row_off, col_off]
    return total

def attend(queries, pairs):
    tokens = queries.shape[0]
    groups = C // (2 * HEAD_DIM)
    qgroup = queries.astype(jnp.float32).reshape(tokens, groups, 2, HEAD_DIM).transpose(1, 0, 2, 3)
    keys = pairs[:, :C // 2].astype(jnp.float32).reshape(-1, groups, HEAD_DIM).transpose(1, 0, 2)
    values = pairs[:, C // 2:].astype(jnp.float32).reshape(-1, groups, HEAD_DIM).transpose(1, 0, 2)

    def one_group(operands):
        qpart, kpart, vpart = operands
        scores = jnp.einsum('tpd,kd->ptk', qpart, kpart) * HEAD_DIM ** (-0.5)
        peak = lax.optimization_barrier(jnp.max(scores, axis=-1, keepdims=True))
        expo = jnp.exp(scores - peak)
        probs = (expo / lax.optimization_barrier(jnp.sum(expo, axis=-1, keepdims=True))).astype(jnp.bfloat16)
        probs = lax.optimization_barrier(probs).astype(jnp.float32)
        return jnp.einsum('ptk,kd->tpd', probs, vpart)
    result = lax.map(one_group, (qgroup, keys, values))
    return result.transpose(1, 0, 2, 3).reshape(tokens, C)

def reference(fields, gain_conv, w_depth, w_layer, gain_attn, gain_out):
    full_w = fields.shape[1]
    bands = fields.shape[0] // LAT_DEV
    sectors = full_w // LON_DEV
    field_float = fields.astype(jnp.float32)
    normed = rms_scale(field_float, gain_conv).astype(jnp.bfloat16)
    normed = lax.optimization_barrier(normed)
    padded = jnp.pad(normed, ((REACH, REACH), (0, 0), (0, 0)))
    padded = jnp.concatenate([padded[:, full_w - REACH:], padded, padded[:, :REACH]], axis=1)

    def one_band(band):
        start = (band * LAT_DEV).astype(jnp.int32)
        slab = lax.dynamic_slice_in_dim(padded, start, LAT_DEV + 2 * REACH, 0)
        own = lax.dynamic_slice_in_dim(field_float, start, LAT_DEV, 0)
        conv_out = depthwise(slab, w_depth, LAT_DEV, full_w).astype(jnp.bfloat16)
        point = jnp.dot(conv_out.reshape(-1, C), w_layer[:, :C], preferred_element_type=jnp.float32)
        mixed = own.reshape(-1, C) + point
        attn_in = rms_scale(mixed, gain_attn).astype(jnp.bfloat16)
        projected = jnp.dot(attn_in, w_layer[:, C:], preferred_element_type=jnp.float32).astype(jnp.bfloat16)
        grid = projected.reshape(LAT_DEV, sectors, LON_DEV, 2 * C).transpose(1, 0, 2, 3)
        grid = grid.reshape(sectors, LAT_DEV * LON_DEV, 2 * C)
        queries = grid[:, :, :C]
        pairs = grid[:, :, C:]
        near = jnp.concatenate([jnp.roll(pairs, offset, axis=0) for offset in (0, 1, 2, -1, -2)], axis=1)
        attended = lax.map(lambda operands: attend(operands[0], operands[1]), (queries, near))
        attended = attended.reshape(sectors, LAT_DEV, LON_DEV, C).transpose(1, 0, 2, 3).reshape(-1, C)
        result = mixed + rms_scale(attended, gain_out)
        return result.astype(jnp.bfloat16).reshape(LAT_DEV, full_w, C)
    outputs = lax.map(one_band, jnp.arange(bands))
    return outputs.reshape(fields.shape[0], full_w, C)
```

```python
import functools

import jax
import jax.numpy as jnp
from jax import lax
from jax.experimental import pallas as pl
from jax.experimental.pallas import tpu as pltpu
from jax.sharding import PartitionSpec as P

C = 1024
KERNEL = 7
REACH = 3
EPS = 1e-06
IN_ROWS = 128
OUT_ROWS = 64
BF = jnp.bfloat16
F32 = jnp.float32


def div(a, b):
    return lax.div(a, jnp.int32(b))


def mod(a, b):
    return lax.rem(a, jnp.int32(b))


def home_device(x, y, z, core):
    return (mod(z, 3) * 4 + x) * 2 + core, y * 4 + div(z, 3)


def work_device(low, half, x, sector):
    y, high = div(sector, 4), mod(sector, 4)
    z = mod(13 - 2 * (2 * low + half) + mod(div(high, 2) + y, 2), 12)
    return home_device(x, y, z, mod(high, 2))


def remote(src, dst, sends, recvs, device):
    return pltpu.make_async_remote_copy(
        src_ref=src,
        dst_ref=dst,
        send_sem=sends,
        recv_sem=recvs,
        device_id=device,
        device_id_type=pl.DeviceIdType.MESH,
    )


def kernel(
    f_ref, gain_conv, w_depth, w_ref, gain_attn, gain_out, out_ref,
    wbuf, pad, normed, lat_in, strip32, strip16, lon_in, conv, mixed, moved_out, moved_in,
    qz, kv, attended, back_out, back_in,
    own_sem, wz_s, wz_r, wx_s, wx_r, wc_s, wc_r, lat_s, lat_r, lon_s, lon_r,
    in_s, in_r, kv_s, kv_r, back_s, back_r,
):
    lat, lon = lax.axis_index("lat"), lax.axis_index("lon")
    core, x, low = mod(lat, 2), mod(div(lat, 2), 4), div(lat, 8)
    y, high = div(lon, 4), mod(lon, 4)
    z = high * 3 + low
    z_next = home_device(x, y, mod(z + 1, 12), core)
    z_prev = home_device(x, y, mod(z + 11, 12), core)
    x_next = ((low * 4 + mod(x + 1, 4)) * 2 + core, lon)
    x_prev = ((low * 4 + mod(x + 3, 4)) * 2 + core, lon)
    partner = (lat + 1 - 2 * core, lon)
    lat_next, lat_prev = (mod(lat + 1, 24), lon), (mod(lat + 23, 24), lon)
    lon_next, lon_prev = (lat, mod(lon + 1, 32)), (lat, mod(lon + 31, 32))
    slot = mod(z + 11, 12)
    pair = mod(6 - div(slot, 2), 6)
    part = mod(mod(slot, 2) + y, 2)
    r_low, r_half = div(pair, 2), mod(pair, 2)
    r_sector = y * 4 + 2 * part + core
    origin = ((r_low * 4 + x) * 2 + r_half, r_sector)
    target = work_device(low, core, x, lon)
    outward = 1 - 2 * core
    near = work_device(r_low, r_half, x, mod(r_sector - outward + 32, 32))
    far = work_device(r_low, r_half, x, mod(r_sector + 2 * outward + 32, 32))
    far_from = work_device(r_low, r_half, x, mod(r_sector - 2 * outward + 32, 32))

    barrier = pltpu.get_barrier_semaphore()
    greeted = (
        z_next, z_prev, x_next, x_prev, partner, lat_next, lat_prev, lon_next, lon_prev,
        origin, target, near, far_from,
    )
    for device in greeted:
        pl.semaphore_signal(
            barrier, inc=1, device_id=device, device_id_type=pl.DeviceIdType.MESH
        )
    pl.semaphore_wait(barrier, len(greeted))

    sent = []

    def go(copy):
        copy.start()
        sent.append(copy)
        return copy

    def block(lo, column):
        return (lo * 4 + mod(column + 4, 4)) * 2 + core

    def wx(lo, way, src=None):
        if way < 2:
            b = block(lo, x)
            source, dst = wbuf.at[b], wbuf.at[b]
        else:
            b = block(lo, x - 1 if way == 2 else x + 1)
            rows = pl.ds(0 if way == 2 else C // 2, C // 2)
            source, dst = wbuf.at[b, rows], wbuf.at[b, rows]
        device = x_next if way % 2 == 0 else x_prev
        return remote(src if src is not None else source, dst, wx_s.at[lo, way], wx_r.at[lo, way], device)

    def wc(lo, step, src=None):
        b = block(lo, x + (0, -1, 1, 2)[step])
        return remote(src if src is not None else wbuf.at[b], wbuf.at[b], wc_s.at[lo, step], wc_r.at[lo, step], partner)

    keep = pltpu.make_async_copy(w_ref, wbuf.at[lat], own_sem)
    keep.start()
    to_next = go(remote(w_ref, wbuf.at[lat], wz_s.at[0], wz_r.at[0], z_next))
    to_prev = go(remote(w_ref, wbuf.at[lat], wz_s.at[1], wz_r.at[1], z_prev))
    go(wx(low, 0, w_ref))
    go(wx(low, 1, w_ref))
    go(wc(low, 0, w_ref))

    def spread(lo):
        go(wx(lo, 0))
        go(wx(lo, 1))
        go(wc(lo, 0))

    def pass_on(lo):
        wx(lo, 0).wait_recv()
        go(wx(lo, 2))
        go(wc(lo, 1))
        wx(lo, 1).wait_recv()
        go(wx(lo, 3))
        go(wc(lo, 2))

    def finish(lo):
        wx(lo, 2).wait_recv()
        wx(lo, 3).wait_recv()
        go(wc(lo, 3))

    def arrived(lo):
        for step in range(4):
            wc(lo, step).wait_recv()

    gain = gain_conv[...]

    def norm_row(row, carry):
        value = f_ref[row].astype(F32)
        mean = jnp.mean(value * value, axis=-1, keepdims=True)
        value = (value * lax.rsqrt(mean + EPS) * gain).astype(BF)
        normed[row] = value
        wide = value.astype(F32)
        for k in range(8):
            pad[k, row + REACH, REACH : REACH + 16, :] = wide[:, k * 128 : (k + 1) * 128]
        return carry

    lax.fori_loop(0, 16, norm_row, 0)

    down = remote(normed.at[pl.ds(13, 3)], lat_in.at[0], lat_s.at[0], lat_r.at[0], lat_next)
    up = remote(normed.at[pl.ds(0, 3)], lat_in.at[1], lat_s.at[1], lat_r.at[1], lat_prev)

    @pl.when(lat < 23)
    def _():
        down.start()

    @pl.when(lat > 0)
    def _():
        up.start()

    for side, here, base in ((0, lat > 0, 0), (1, lat < 23, 19)):
        copy = down if side == 0 else up

        @pl.when(here)
        def _():
            copy.wait_recv()
            for row in range(3):
                wide = lat_in[side, row].astype(F32)
                for k in range(8):
                    pad[k, base + row, REACH : REACH + 16, :] = wide[:, k * 128 : (k + 1) * 128]

        @pl.when(jnp.logical_not(here))
        def _():
            for row in range(3):
                for k in range(8):
                    pad[k, base + row, REACH : REACH + 16, :] = jnp.zeros((16, 128), F32)

    strip32[pl.ds(64, 16), :] = jnp.zeros((16, C), F32)
    lon_copies = []
    for side, first, device in ((0, 16, lon_next), (1, REACH, lon_prev)):
        for row in range(22):
            for k in range(8):
                strip32[pl.ds(row * 3, 3), k * 128 : (k + 1) * 128] = pad[k, row, first : first + 3, :]
        strip16[side] = strip32[...].astype(BF)
        lon_copies.append(go(remote(strip16.at[side], lon_in.at[side], lon_s.at[side], lon_r.at[side], device)))

    keep.wait()
    to_next.wait_recv()
    to_prev.wait_recv()
    spread(mod(low + 1, 3))
    spread(mod(low + 2, 3))
    pass_on(0)

    for side, first in ((0, 0), (1, 19)):
        lon_copies[side].wait_recv()
        strip32[...] = lon_in[side].astype(F32)
        for row in range(22):
            for k in range(8):
                pad[k, row, first : first + 3, :] = strip32[pl.ds(row * 3, 3), k * 128 : (k + 1) * 128]

    def depthwise(top):
        def lanes(k, carry):
            at = pl.multiple_of(k * 128, 128)
            total = [None] * 8
            for b in range(KERNEL):
                for row in range(8 + 2 * REACH):
                    value = pad[k, top + row, b : b + 16, :]
                    for a in range(KERNEL):
                        i = row - a
                        if 0 <= i < 8:
                            term = value * w_depth[a, b : b + 1, pl.ds(at, 128)]
                            total[i] = term if total[i] is None else total[i] + term
            for i in range(8):
                conv[pl.ds((top + i) * 16, 16), pl.ds(at, 128)] = total[i].astype(BF)
            return carry

        lax.fori_loop(0, 8, lanes, 0)

    def weights(n):
        return jnp.concatenate([wbuf[2 * n], wbuf[2 * n + 1]], axis=1)

    def pointwise(start):
        rows = pl.ds(start, IN_ROWS)
        value = conv[rows, :]

        def columns(n, carry):
            at = pl.ds(pl.multiple_of(n * 256, 256), 256)
            own = f_ref[pl.ds(start // 16, IN_ROWS // 16), :, at].reshape(IN_ROWS, 256)
            mixed[rows, at] = own.astype(F32) + jnp.dot(value, weights(n), preferred_element_type=F32)
            return carry

        lax.fori_loop(0, 4, columns, 0)

    attn_gain = gain_attn[...]

    def attn_norm(start):
        def some(n, carry):
            rows = pl.ds(pl.multiple_of(start + n * 32, 32), 32)
            value = mixed[rows, :]
            mean = jnp.mean(value * value, axis=-1, keepdims=True)
            moved_out[rows, :] = (value * lax.rsqrt(mean + EPS) * attn_gain).astype(BF)
            return carry

        lax.fori_loop(0, IN_ROWS // 32, some, 0)

    depthwise(0)
    finish(0)
    pass_on(2)
    arrived(0)
    moves = []
    for i in range(256 // IN_ROWS):
        if i:
            depthwise(i * IN_ROWS // 16)
        pointwise(i * IN_ROWS)
        attn_norm(i * IN_ROWS)
        rows = pl.ds(i * IN_ROWS, IN_ROWS)
        moves.append(go(remote(moved_out.at[rows], moved_in.at[rows], in_s.at[i], in_r.at[i], target)))

    finish(2)
    pass_on(1)
    arrived(2)

    pieces = []
    for i in range(256 // IN_ROWS):
        rows = pl.ds(i * IN_ROWS, IN_ROWS)
        moves[i].wait_recv()
        value = moved_in[rows, :]

        def columns(n, carry):
            at = pl.ds(pl.multiple_of(n * 256, 256), 256)
            kv[0, rows, at] = jnp.dot(value, weights(n + 8), preferred_element_type=F32).astype(BF)
            return carry

        lax.fori_loop(0, 4, columns, 0)
        pieces.append(
            [
                go(remote(kv.at[0, rows], kv.at[to, rows], kv_s.at[i, to], kv_r.at[i, to], device))
                for to, device in ((3, near), (2, far), (1, partner))
            ]
        )

    finish(1)
    arrived(1)

    left_half = lax.broadcasted_iota(jnp.int32, (256, 128), 1) < 64

    def queries(i, carry):
        value = jnp.dot(moved_in[...], weights(i + 4), preferred_element_type=F32)
        value = value.astype(BF).astype(F32) * 0.125
        first, second = value[:, :128], value[:, 128:]
        zero = jnp.zeros_like(first)
        qz[i, 0] = jnp.where(left_half, first, zero).astype(BF)
        qz[i, 1] = jnp.where(left_half, pltpu.roll(first, 64, 1), zero).astype(BF)
        qz[i, 2] = jnp.where(left_half, zero, pltpu.roll(second, 64, 1)).astype(BF)
        qz[i, 3] = jnp.where(left_half, zero, second).astype(BF)
        return carry

    lax.fori_loop(0, 4, queries, 0)

    for i, (to_near, to_far, to_partner) in enumerate(pieces):
        rows = pl.ds(i * IN_ROWS, IN_ROWS)
        to_near.wait_recv()
        to_near = go(remote(kv.at[3, rows], kv.at[4, rows], kv_s.at[i, 4], kv_r.at[i, 4], partner))
        pieces[i].append(to_near)
    for _, to_far, to_partner, relayed in pieces:
        to_far.wait_recv()
        to_partner.wait_recv()
        relayed.wait_recv()

    out_gain = gain_out[...]
    half = lax.broadcasted_iota(jnp.int32, (OUT_ROWS, 128), 1) < 64

    def attend(start):
        rows = pl.ds(start, OUT_ROWS)

        def heads(i, carry):
            at = pl.ds(pl.multiple_of(i * 128, 128), 128)
            values_at = pl.ds(pl.multiple_of(i * 128 + C // 2, 128), 128)
            query = qz[i, :, rows, :].reshape(4 * OUT_ROWS, 128)
            keys = kv[:, :, at].reshape(1280, 128)
            values = kv[:, :, values_at].reshape(1280, 128)
            scores = lax.dot_general(query, keys, (((1,), (1,)), ((), ())), preferred_element_type=F32)
            peak = jnp.max(scores, axis=-1, keepdims=True)
            expo = jnp.exp(scores - peak).astype(BF)
            wide = jnp.concatenate([values, jnp.ones((1280, 128), BF)], axis=1)
            both = jnp.dot(expo, wide, preferred_element_type=F32)
            result = (both[:, :128] / both[:, 128:]).reshape(4, OUT_ROWS, 128)
            first = jnp.where(half, result[0], pltpu.roll(result[1], 64, 1))
            second = jnp.where(half, pltpu.roll(result[2], 64, 1), result[3])
            out_at = pl.multiple_of(i * 256, 256)
            attended[:, pl.ds(out_at, 128)] = first
            attended[:, pl.ds(out_at + 128, 128)] = second
            return carry

        lax.fori_loop(0, 4, heads, 0)
        value = attended[...]
        mean = jnp.mean(value * value, axis=-1, keepdims=True)
        back_out[rows, :] = (value * lax.rsqrt(mean + EPS) * out_gain).astype(BF)

    backs = []
    for i in range(256 // OUT_ROWS):
        attend(i * OUT_ROWS)
        rows = pl.ds(i * OUT_ROWS, OUT_ROWS)
        backs.append(go(remote(back_out.at[rows], back_in.at[rows], back_s.at[i], back_r.at[i], origin)))
    for i, copy in enumerate(backs):
        rows = pl.ds(i * OUT_ROWS, OUT_ROWS)
        copy.wait_recv()
        total = mixed[rows, :] + back_in[rows, :].astype(F32)
        out_ref[pl.ds(i * OUT_ROWS // 16, OUT_ROWS // 16)] = total.astype(BF).reshape(OUT_ROWS // 16, 16, C)

    for copy in sent:
        copy.wait_send()

    @pl.when(lat < 23)
    def _():
        down.wait_send()

    @pl.when(lat > 0)
    def _():
        up.wait_send()


def per_device(fields, gain_conv, w_depth, w_layer, gain_attn, gain_out):
    vmem = pl.BlockSpec(memory_space=pltpu.VMEM)
    dma = pltpu.SemaphoreType.DMA
    n_in, n_out = 256 // IN_ROWS, 256 // OUT_ROWS
    return pl.pallas_call(
        kernel,
        out_shape=jax.ShapeDtypeStruct(fields.shape, BF),
        in_specs=[vmem, vmem, vmem, pl.BlockSpec(memory_space=pl.ANY), vmem, vmem],
        out_specs=vmem,
        scratch_shapes=[
            pltpu.VMEM((24, C, 128), BF),
            pltpu.VMEM((8, 22, 24, 128), F32),
            pltpu.VMEM((16, 16, C), BF),
            pltpu.VMEM((2, 3, 16, C), BF),
            pltpu.VMEM((80, C), F32),
            pltpu.VMEM((2, 80, C), BF),
            pltpu.VMEM((2, 80, C), BF),
            pltpu.VMEM((256, C), BF),
            pltpu.VMEM((256, C), F32),
            pltpu.VMEM((256, C), BF),
            pltpu.VMEM((256, C), BF),
            pltpu.VMEM((4, 4, 256, 128), BF),
            pltpu.VMEM((5, 256, C), BF),
            pltpu.VMEM((OUT_ROWS, C), F32),
            pltpu.VMEM((256, C), BF),
            pltpu.VMEM((256, C), BF),
            dma,
            dma((2,)), dma((2,)),
            dma((3, 4)), dma((3, 4)),
            dma((3, 4)), dma((3, 4)),
            dma((2,)), dma((2,)),
            dma((2,)), dma((2,)),
            dma((n_in,)), dma((n_in,)),
            dma((n_in, 5)), dma((n_in, 5)),
            dma((n_out,)), dma((n_out,)),
        ],
        compiler_params=pltpu.CompilerParams(
            collective_id=0, has_side_effects=True, vmem_limit_bytes=60 * 1024 * 1024
        ),
        name="layer",
    )(
        fields, gain_conv.reshape(1, C), w_depth, w_layer,
        gain_attn.reshape(1, C), gain_out.reshape(1, C),
    )


def solution(mesh):
    return jax.shard_map(
        per_device,
        mesh=mesh,
        in_specs=(P("lat", "lon", None), P(), P(), P(None, "lat"), P(), P()),
        out_specs=P("lat", "lon", None),
        check_vma=False,
    )
```

```python
import functools

import jax
import jax.numpy as jnp
from jax import lax
from jax.experimental import pallas as pl
from jax.experimental.pallas import tpu as pltpu
from jax.sharding import PartitionSpec as P

C = 1024
KERNEL = 7
REACH = 3
EPS = 1e-06
MIX_ROWS = 128
IN_ROWS = 64
OUT_ROWS = (32, 32, 64, 64, 64)
BF = jnp.bfloat16
F32 = jnp.float32


def div(a, b):
    return lax.div(a, jnp.int32(b))


def mod(a, b):
    return lax.rem(a, jnp.int32(b))


def home_device(x, y, z, core):
    return (mod(z, 3) * 4 + x) * 2 + core, y * 4 + div(z, 3)


BAND_Z = (10, 7, 11, 5, 8, 2, 3, 9, 1, 4, 6, 0)
BAND_FLIP = (0, 0, 1, 1, 1, 0, 0, 0, 1, 1, 0, 0)


def pick(table, index):
    value = jnp.int32(0)
    for i, entry in enumerate(table):
        if entry:
            value = value + jnp.where(index == i, jnp.int32(entry), jnp.int32(0))
    return value


def work_device(band, x_pair, sector):
    y, high = div(sector, 4), mod(sector, 4)
    x = 2 * x_pair + mod(div(high, 2) + y + pick(BAND_FLIP, band), 2)
    return home_device(x, y, pick(BAND_Z, band), mod(high, 2))


def remote(src, dst, sends, recvs, device):
    return pltpu.make_async_remote_copy(
        src_ref=src,
        dst_ref=dst,
        send_sem=sends,
        recv_sem=recvs,
        device_id=device,
        device_id_type=pl.DeviceIdType.MESH,
    )


def kernel(
    f_ref, gain_conv, w_depth, w_ref, gain_attn, gain_out, mixed, back_in,
    wbuf, pad, edge, inner, normed, lat_in, strip32, strip16, lon_in, corner_out, corner_in, conv, moved_out, moved_in,
    qz, kv, attended, back_out,
    own_sem, wz_s, wz_r, wx_s, wx_r, wy_s, wy_r, wc_s, wc_r, lat_s, lat_r, lon_s, lon_r, corner_s, corner_r,
    in_s, in_r, kv_s, kv_r, back_s, back_r,
):
    lat, lon = lax.axis_index("lat"), lax.axis_index("lon")
    core, x, low = mod(lat, 2), mod(div(lat, 2), 4), div(lat, 8)
    y, high = div(lon, 4), mod(lon, 4)
    z = high * 3 + low
    z_next = home_device(x, y, mod(z + 1, 12), core)
    z_prev = home_device(x, y, mod(z + 11, 12), core)
    x_next = ((low * 4 + mod(x + 1, 4)) * 2 + core, lon)
    x_prev = ((low * 4 + mod(x + 3, 4)) * 2 + core, lon)
    partner = (lat + 1 - 2 * core, lon)
    lat_next, lat_prev = (mod(lat + 1, 24), lon), (mod(lat + 23, 24), lon)
    lon_next, lon_prev = (lat, mod(lon + 1, 32)), (lat, mod(lon + 31, 32))
    y_next, y_prev = (lat, mod(lon + 4, 32)), (lat, mod(lon + 28, 32))
    x_pair = div(x, 2)
    band = pick([BAND_Z.index(i) for i in range(12)], z)
    part = mod(mod(x, 2) + y + pick(BAND_FLIP, band), 2)
    sector = y * 4 + 2 * part + core
    origin = ((div(band, 4) * 4 + 2 * x_pair + mod(div(band, 2), 2)) * 2 + mod(band, 2), sector)
    target = work_device(low * 4 + mod(x, 2) * 2 + core, x_pair, lon)
    outward = 1 - 2 * core
    near = work_device(band, x_pair, mod(sector - outward + 32, 32))
    far = work_device(band, x_pair, mod(sector + 2 * outward + 32, 32))
    far_from = work_device(band, x_pair, mod(sector - 2 * outward + 32, 32))

    barrier = pltpu.get_barrier_semaphore()
    greeted = (
        z_next, z_prev, x_next, x_prev, y_next, y_prev, partner, lat_next, lat_prev, lon_next, lon_prev,
        origin, target, near, far_from,
    )
    for device in greeted:
        pl.semaphore_signal(
            barrier, inc=1, device_id=device, device_id_type=pl.DeviceIdType.MESH
        )

    def clear(row, carry):
        zero = jnp.zeros((8, 128), F32)
        for k in range(8):
            for first in (0, 16):
                pad[k, row, first : first + 8, :] = zero
            for side in range(2):
                for first in (0, 8):
                    edge[side, k, row, first : first + 8, :] = zero
        return carry

    lax.fori_loop(0, 22, clear, 0)
    pl.semaphore_wait(barrier, len(greeted))

    sent = []

    def go(copy):
        copy.start()
        sent.append(copy)
        return copy

    HALF, QUARTER = C // 2, C // 4
    mine = pl.multiple_of(mod(y, 2) * HALF, HALF)

    def block(lo, step):
        return (lo * 4 + mod(x + (0, 3, 1, 2)[step], 4)) * 2 + core

    def wx(lo, way, src=None):
        b = block(lo, (0, 0, 1, 2)[way])
        rows = (pl.ds(mine, HALF), pl.ds(mine, HALF), pl.ds(mine, QUARTER), pl.ds(mine + QUARTER, QUARTER))[way]
        piece = wbuf.at[b, rows]
        source = piece if src is None else src.at[rows]
        return remote(source, piece, wx_s.at[lo, way], wx_r.at[lo, way], x_prev if way % 2 else x_next)

    def wy(lo, step, way):
        piece = wbuf.at[block(lo, step), pl.ds(mine + way * QUARTER, QUARTER)]
        at = step * 2 + way
        return remote(piece, piece, wy_s.at[lo, at], wy_r.at[lo, at], y_next if way else y_prev)

    def wc(lo, step, src=None):
        piece = wbuf.at[block(lo, step)]
        return remote(piece if src is None else src, piece, wc_s.at[lo, step], wc_r.at[lo, step], partner)

    keep = pltpu.make_async_copy(w_ref, wbuf.at[lat], own_sem)
    keep.start()
    own_half, there = w_ref.at[pl.ds(mine, HALF)], wbuf.at[lat, pl.ds(mine, HALF)]
    go(remote(own_half, there, wz_s.at[0], wz_r.at[0], z_next))
    go(remote(own_half, there, wz_s.at[1], wz_r.at[1], z_prev))
    for copy in (wx(low, 0, w_ref), wx(low, 1, w_ref), wc(low, 0, w_ref)):
        copy.start()
    for lo in range(3):
        sent.extend((wx(lo, 0), wx(lo, 1), wc(lo, 0)))

    def spread(lo):
        @pl.when(low != lo)
        def _():
            side = 2 - mod(lo - low + 3, 3)
            here = wbuf.at[block(lo, 0), pl.ds(mine, HALF)]
            remote(own_half, here, wz_s.at[0], wz_r.at[side], z_next).wait_recv()
            for copy in (wx(lo, 0), wx(lo, 1), wy(lo, 0, 0), wy(lo, 0, 1)):
                copy.start()

    def pass_on(lo):
        for way in range(2):
            wx(lo, way).wait_recv()
            go(wx(lo, 2 + way))
            go(wy(lo, 1 + way, 0))
            go(wy(lo, 1 + way, 1))

    def relay(lo):
        wx(lo, 2).wait_recv()
        wx(lo, 3).wait_recv()
        go(wy(lo, 3, 0))
        go(wy(lo, 3, 1))

    def finish(lo):
        @pl.when(low != lo)
        def _():
            wy(lo, 0, 0).wait_recv()
            wy(lo, 0, 1).wait_recv()
            wc(lo, 0).start()

        for step in range(1, 4):
            wy(lo, step, 0).wait_recv()
            wy(lo, step, 1).wait_recv()
            go(wc(lo, step))

    def arrived(lo):
        for step in range(4):
            wc(lo, step).wait_recv()

    gain = gain_conv[...]

    def norm_row(row, carry):
        value = f_ref[row].astype(F32)
        mean = jnp.mean(value * value, axis=-1, keepdims=True)
        value = (value * lax.rsqrt(mean + EPS) * gain).astype(BF)
        normed[row] = value
        wide = value.astype(F32)
        for k in range(8):
            pad[k, row + REACH, REACH : REACH + 16, :] = wide[:, k * 128 : (k + 1) * 128]
        return carry

    lax.fori_loop(0, 16, norm_row, 0)

    down = remote(normed.at[pl.ds(13, 3)], lat_in.at[0], lat_s.at[0], lat_r.at[0], lat_next)
    up = remote(normed.at[pl.ds(0, 3)], lat_in.at[1], lat_s.at[1], lat_r.at[1], lat_prev)

    @pl.when(lat < 23)
    def _():
        down.start()

    @pl.when(lat > 0)
    def _():
        up.start()

    sides = ((0, 16, lon_next), (1, REACH, lon_prev))
    lon_copies, corner_copies = [], []
    for side, first, device in sides:
        for row in range(16):
            for k in range(8):
                strip32[pl.ds(row * 3, 3), k * 128 : (k + 1) * 128] = pad[k, row + REACH, first : first + 3, :]
        strip16[side] = strip32[...].astype(BF)
        lon_copies.append(go(remote(strip16.at[side], lon_in.at[side], lon_s.at[side], lon_r.at[side], device)))

    for side, here, base in ((0, lat > 0, 0), (1, lat < 23, 19)):
        copy = down if side == 0 else up

        @pl.when(here)
        def _():
            copy.wait_recv()
            for row in range(3):
                wide = lat_in[side, row].astype(F32)
                for k in range(8):
                    pad[k, base + row, REACH : REACH + 16, :] = wide[:, k * 128 : (k + 1) * 128]

        @pl.when(jnp.logical_not(here))
        def _():
            for row in range(3):
                for k in range(8):
                    pad[k, base + row, REACH : REACH + 16, :] = jnp.zeros((16, 128), F32)

    strip32[pl.ds(16, 8), :] = jnp.zeros((8, C), F32)
    for side, first, device in sides:
        for n in range(6):
            row = n if n < 3 else n + 16
            for k in range(8):
                strip32[pl.ds(n * 3, 3), k * 128 : (k + 1) * 128] = pad[k, row, first : first + 3, :]
        corner_out[side] = strip32[pl.ds(0, 24), :].astype(BF)
        corner_copies.append(
            go(remote(corner_out.at[side], corner_in.at[side], corner_s.at[side], corner_r.at[side], device))
        )

    deep = 8

    def depthwise(top):
        def lanes(k, carry):
            at = pl.multiple_of(k * 128, 128)
            total = [None] * deep
            for b in range(KERNEL):
                for row in range(deep + 2 * REACH):
                    value = pad[k, top + row, b : b + 16, :]
                    for a in range(KERNEL):
                        i = row - a
                        if 0 <= i < deep:
                            term = value * w_depth[a, b : b + 1, pl.ds(at, 128)]
                            total[i] = term if total[i] is None else total[i] + term
            for i in range(deep):
                inner[k, top + i] = total[i]
            return carry

        lax.fori_loop(0, 8, lanes, 0)

    def neighbours(top):
        def lanes(k, carry):
            at = pl.multiple_of(k * 128, 128)
            total = [[inner[k, top + i, side * 8 : side * 8 + 8, :] for i in range(deep)] for side in range(2)]
            for side in range(2):
                for shift in range(REACH):
                    b = shift + 4 * side
                    for row in range(deep + 2 * REACH):
                        value = edge[side, k, top + row, shift : shift + 8, :]
                        for a in range(KERNEL):
                            i = row - a
                            if 0 <= i < deep:
                                total[side][i] += value * w_depth[a, b : b + 1, pl.ds(at, 128)]
            for i in range(deep):
                both = jnp.concatenate([total[0][i], total[1][i]], axis=0)
                conv[pl.ds((top + i) * 16, 16), pl.ds(at, 128)] = both.astype(BF)
            return carry

        lax.fori_loop(0, 8, lanes, 0)

    def weights(n):
        return jnp.concatenate([wbuf[2 * n], wbuf[2 * n + 1]], axis=1)

    def pointwise(start):
        rows = pl.ds(start, MIX_ROWS)
        value = conv[rows, :]

        def columns(n, carry):
            at = pl.ds(pl.multiple_of(n * 256, 256), 256)
            own = f_ref[pl.ds(start // 16, MIX_ROWS // 16), :, at].reshape(MIX_ROWS, 256)
            mixed[rows, at] = own.astype(F32) + jnp.dot(value, weights(n), preferred_element_type=F32)
            return carry

        lax.fori_loop(0, 4, columns, 0)

    attn_gain = gain_attn[...]

    def attn_norm(start):
        def some(n, carry):
            rows = pl.ds(pl.multiple_of(start + n * 32, 32), 32)
            value = mixed[rows, :]
            mean = jnp.mean(value * value, axis=-1, keepdims=True)
            moved_out[rows, :] = (value * lax.rsqrt(mean + EPS) * attn_gain).astype(BF)
            return carry

        lax.fori_loop(0, IN_ROWS // 32, some, 0)

    spread(0)
    depthwise(0)
    pass_on(0)
    depthwise(deep)
    spread(2)
    spread(1)
    relay(0)
    keep.wait()
    for side, first in ((0, 0), (1, 7)):
        lon_copies[side].wait_recv()
        strip32[...] = lon_in[side].astype(F32)
        for row in range(16):
            for k in range(8):
                edge[side, k, row + REACH, first : first + 3, :] = strip32[pl.ds(row * 3, 3), k * 128 : (k + 1) * 128]
    for side, first in ((0, 0), (1, 7)):
        corner_copies[side].wait_recv()
        strip32[pl.ds(0, 24), :] = corner_in[side].astype(F32)
        for n in range(6):
            row = n if n < 3 else n + 16
            for k in range(8):
                edge[side, k, row, first : first + 3, :] = strip32[pl.ds(n * 3, 3), k * 128 : (k + 1) * 128]
    neighbours(0)
    finish(0)
    neighbours(deep)
    pass_on(2)
    relay(2)
    arrived(0)
    moves = []
    for i in range(256 // MIX_ROWS):
        pointwise(i * MIX_ROWS)
        for j in range(i * MIX_ROWS // IN_ROWS, (i + 1) * MIX_ROWS // IN_ROWS):
            attn_norm(j * IN_ROWS)
            rows = pl.ds(j * IN_ROWS, IN_ROWS)
            moves.append(go(remote(moved_out.at[rows], moved_in.at[rows], in_s.at[j], in_r.at[j], target)))

    finish(2)
    pass_on(1)
    relay(1)
    arrived(2)

    pieces = []
    for i in range(256 // IN_ROWS):
        rows = pl.ds(i * IN_ROWS, IN_ROWS)
        moves[i].wait_recv()
        value = moved_in[rows, :]

        def columns(n, carry):
            at = pl.ds(pl.multiple_of(n * 256, 256), 256)
            kv[0, rows, at] = jnp.dot(value, weights(n + 8), preferred_element_type=F32).astype(BF)
            return carry

        lax.fori_loop(0, 4, columns, 0)
        pieces.append(
            [
                go(remote(kv.at[0, rows], kv.at[to, rows], kv_s.at[i, to], kv_r.at[i, to], device))
                for to, device in ((3, near), (2, far), (1, partner))
            ]
        )

    finish(1)
    arrived(1)

    left_half = lax.broadcasted_iota(jnp.int32, (256, 128), 1) < 64

    def queries(i, carry):
        value = jnp.dot(moved_in[...], weights(i + 4), preferred_element_type=F32)
        value = value.astype(BF).astype(F32) * 0.125
        first, second = value[:, :128], value[:, 128:]
        zero = jnp.zeros_like(first)
        qz[i, 0] = jnp.where(left_half, first, zero).astype(BF)
        qz[i, 1] = jnp.where(left_half, pltpu.roll(first, 64, 1), zero).astype(BF)
        qz[i, 2] = jnp.where(left_half, zero, pltpu.roll(second, 64, 1)).astype(BF)
        qz[i, 3] = jnp.where(left_half, zero, second).astype(BF)
        return carry

    lax.fori_loop(0, 4, queries, 0)

    for i, (to_near, to_far, to_partner) in enumerate(pieces):
        rows = pl.ds(i * IN_ROWS, IN_ROWS)
        to_near.wait_recv()
        to_near = go(remote(kv.at[3, rows], kv.at[4, rows], kv_s.at[i, 4], kv_r.at[i, 4], partner))
        pieces[i].append(to_near)
    for _, to_far, to_partner, relayed in pieces:
        to_far.wait_recv()
        to_partner.wait_recv()
        relayed.wait_recv()

    out_gain = gain_out[...]
    def attend(start, size):
        rows = pl.ds(start, size)
        half = lax.broadcasted_iota(jnp.int32, (size, 128), 1) < 64

        def heads(i, carry):
            at = pl.ds(pl.multiple_of(i * 128, 128), 128)
            values_at = pl.ds(pl.multiple_of(i * 128 + C // 2, 128), 128)
            query = qz[i, :, rows, :].reshape(4 * size, 128)
            keys = kv[:, :, at].reshape(1280, 128)
            values = kv[:, :, values_at].reshape(1280, 128)
            scores = lax.dot_general(query, keys, (((1,), (1,)), ((), ())), preferred_element_type=F32)
            peak = jnp.max(scores, axis=-1, keepdims=True)
            expo = jnp.exp(scores - peak).astype(BF)
            wide = jnp.concatenate([values, jnp.ones((1280, 128), BF)], axis=1)
            both = jnp.dot(expo, wide, preferred_element_type=F32)
            result = (both[:, :128] / both[:, 128:]).reshape(4, size, 128)
            first = jnp.where(half, result[0], pltpu.roll(result[1], 64, 1))
            second = jnp.where(half, pltpu.roll(result[2], 64, 1), result[3])
            out_at = pl.multiple_of(i * 256, 256)
            attended[pl.ds(0, size), pl.ds(out_at, 128)] = first
            attended[pl.ds(0, size), pl.ds(out_at + 128, 128)] = second
            return carry

        lax.fori_loop(0, 4, heads, 0)
        value = attended[pl.ds(0, size), :]
        mean = jnp.mean(value * value, axis=-1, keepdims=True)
        back_out[rows, :] = (value * lax.rsqrt(mean + EPS) * out_gain).astype(BF)

    backs, start = [], 0
    for i, size in enumerate(OUT_ROWS):
        attend(start, size)
        rows = pl.ds(start, size)
        backs.append(go(remote(back_out.at[rows], back_in.at[rows], back_s.at[i], back_r.at[i], origin)))
        start += size
    for copy in backs:
        copy.wait_recv()

    for copy in sent:
        copy.wait_send()
    for lo in range(3):

        @pl.when(low != lo)
        def _():
            wy(lo, 0, 0).wait_send()
            wy(lo, 0, 1).wait_send()

    @pl.when(lat < 23)
    def _():
        down.wait_send()

    @pl.when(lat > 0)
    def _():
        up.wait_send()


def per_device(fields, gain_conv, w_depth, w_layer, gain_attn, gain_out):
    vmem = pl.BlockSpec(memory_space=pltpu.VMEM)
    dma = pltpu.SemaphoreType.DMA
    n_in, n_out = 256 // IN_ROWS, len(OUT_ROWS)
    mixed, back = pl.pallas_call(
        kernel,
        out_shape=[jax.ShapeDtypeStruct((256, C), F32), jax.ShapeDtypeStruct((256, C), BF)],
        in_specs=[vmem, vmem, vmem, pl.BlockSpec(memory_space=pl.ANY), vmem, vmem],
        out_specs=[vmem, vmem],
        scratch_shapes=[
            pltpu.VMEM((24, C, 128), BF),
            pltpu.VMEM((8, 22, 24, 128), F32),
            pltpu.VMEM((2, 8, 22, 16, 128), F32),
            pltpu.VMEM((8, 16, 16, 128), F32),
            pltpu.VMEM((16, 16, C), BF),
            pltpu.VMEM((2, 3, 16, C), BF),
            pltpu.VMEM((48, C), F32),
            pltpu.VMEM((2, 48, C), BF),
            pltpu.VMEM((2, 48, C), BF),
            pltpu.VMEM((2, 24, C), BF),
            pltpu.VMEM((2, 24, C), BF),
            pltpu.VMEM((256, C), BF),
            pltpu.VMEM((256, C), BF),
            pltpu.VMEM((256, C), BF),
            pltpu.VMEM((4, 4, 256, 128), BF),
            pltpu.VMEM((5, 256, C), BF),
            pltpu.VMEM((max(OUT_ROWS), C), F32),
            pltpu.VMEM((256, C), BF),
            dma,
            dma((2,)), dma((2,)),
            dma((3, 4)), dma((3, 4)),
            dma((3, 8)), dma((3, 8)),
            dma((3, 4)), dma((3, 4)),
            dma((2,)), dma((2,)),
            dma((2,)), dma((2,)),
            dma((2,)), dma((2,)),
            dma((n_in,)), dma((n_in,)),
            dma((n_in, 5)), dma((n_in, 5)),
            dma((n_out,)), dma((n_out,)),
        ],
        compiler_params=pltpu.CompilerParams(
            collective_id=0, has_side_effects=True, vmem_limit_bytes=60 * 1024 * 1024
        ),
        name="layer",
    )(
        fields, gain_conv.reshape(1, C), w_depth, w_layer,
        gain_attn.reshape(1, C), gain_out.reshape(1, C),
    )
    return (mixed + back.astype(F32)).astype(BF).reshape(fields.shape)


def solution(mesh):
    return jax.shard_map(
        per_device,
        mesh=mesh,
        in_specs=(P("lat", "lon", None), P(), P(), P(None, "lat"), P(), P()),
        out_specs=P("lat", "lon", None),
        check_vma=False,
    )
```

```python
import functools

import jax
import jax.numpy as jnp
from jax import lax
from jax.experimental import pallas as pl
from jax.experimental.pallas import tpu as pltpu
from jax.sharding import PartitionSpec as P

C = 1024
KERNEL = 7
REACH = 3
EPS = 1e-06
MIX_ROWS = 128
IN_ROWS = 64
OUT_ROWS = (32, 32, 64, 64, 64)
BF = jnp.bfloat16
F32 = jnp.float32


def div(a, b):
    return lax.div(a, jnp.int32(b))


def mod(a, b):
    return lax.rem(a, jnp.int32(b))


def home_device(x, y, z, core):
    return (mod(z, 3) * 4 + x) * 2 + core, y * 4 + div(z, 3)


BAND_Z = (10, 7, 11, 5, 8, 2, 3, 9, 1, 4, 6, 0)
BAND_FLIP = (0, 0, 1, 1, 1, 0, 0, 0, 1, 1, 0, 0)


def pick(table, index):
    value = jnp.int32(0)
    for i, entry in enumerate(table):
        if entry:
            value = value + jnp.where(index == i, jnp.int32(entry), jnp.int32(0))
    return value


def work_device(band, x_pair, sector):
    y, high = div(sector, 4), mod(sector, 4)
    x = 2 * x_pair + mod(div(high, 2) + y + pick(BAND_FLIP, band), 2)
    return home_device(x, y, pick(BAND_Z, band), mod(high, 2))


def remote(src, dst, sends, recvs, device):
    return pltpu.make_async_remote_copy(
        src_ref=src,
        dst_ref=dst,
        send_sem=sends,
        recv_sem=recvs,
        device_id=device,
        device_id_type=pl.DeviceIdType.MESH,
    )


def kernel(
    f_ref, gain_conv, w_depth, w_ref, gain_attn, gain_out, mixed, back_in,
    wbuf, pad, edge, inner, normed, lat_in, strip32, strip16, lon_in, corner_out, corner_in, conv, moved_out, moved_in,
    qz, kv, attended, back_out,
    own_sem, wz_s, wz_r, wx_s, wx_r, wy_s, wy_r, wc_s, wc_r, lat_s, lat_r, lon_s, lon_r, corner_s, corner_r,
    in_s, in_r, kv_s, kv_r, back_s, back_r,
):
    lat, lon = lax.axis_index("lat"), lax.axis_index("lon")
    core, x, low = mod(lat, 2), mod(div(lat, 2), 4), div(lat, 8)
    y, high = div(lon, 4), mod(lon, 4)
    z = high * 3 + low
    z_next = home_device(x, y, mod(z + 1, 12), core)
    z_prev = home_device(x, y, mod(z + 11, 12), core)
    x_next = ((low * 4 + mod(x + 1, 4)) * 2 + core, lon)
    x_prev = ((low * 4 + mod(x + 3, 4)) * 2 + core, lon)
    partner = (lat + 1 - 2 * core, lon)
    lat_next, lat_prev = (mod(lat + 1, 24), lon), (mod(lat + 23, 24), lon)
    lon_next, lon_prev = (lat, mod(lon + 1, 32)), (lat, mod(lon + 31, 32))
    y_next, y_prev = (lat, mod(lon + 4, 32)), (lat, mod(lon + 28, 32))
    x_pair = div(x, 2)
    band = pick([BAND_Z.index(i) for i in range(12)], z)
    part = mod(mod(x, 2) + y + pick(BAND_FLIP, band), 2)
    sector = y * 4 + 2 * part + core
    origin = ((div(band, 4) * 4 + 2 * x_pair + mod(div(band, 2), 2)) * 2 + mod(band, 2), sector)
    target = work_device(low * 4 + mod(x, 2) * 2 + core, x_pair, lon)
    outward = 1 - 2 * core
    near = work_device(band, x_pair, mod(sector - outward + 32, 32))
    far = work_device(band, x_pair, mod(sector + 2 * outward + 32, 32))
    far_from = work_device(band, x_pair, mod(sector - 2 * outward + 32, 32))

    barrier = pltpu.get_barrier_semaphore()
    greeted = (
        z_next, z_prev, x_next, x_prev, y_next, y_prev, partner, lat_next, lat_prev, lon_next, lon_prev,
        origin, target, near, far_from,
    )
    for device in greeted:
        pl.semaphore_signal(
            barrier, inc=1, device_id=device, device_id_type=pl.DeviceIdType.MESH
        )

    def clear(row, carry):
        zero = jnp.zeros((8, 128), F32)
        for k in range(8):
            for first in (0, 16):
                pad[k, row, first : first + 8, :] = zero
            for side in range(2):
                for first in (0, 8):
                    edge[side, k, row, first : first + 8, :] = zero
        return carry

    lax.fori_loop(0, 22, clear, 0)
    pl.semaphore_wait(barrier, len(greeted))

    sent = []

    def go(copy):
        copy.start()
        sent.append(copy)
        return copy

    HALF, QUARTER = C // 2, C // 4
    mine = pl.multiple_of(mod(y, 2) * HALF, HALF)

    def block(lo, step):
        return (lo * 4 + mod(x + (0, 3, 1, 2)[step], 4)) * 2 + core

    def wx(lo, way, src=None):
        b = block(lo, (0, 0, 1, 2)[way])
        rows = (pl.ds(mine, HALF), pl.ds(mine, HALF), pl.ds(mine, QUARTER), pl.ds(mine + QUARTER, QUARTER))[way]
        piece = wbuf.at[b, rows]
        source = piece if src is None else src.at[rows]
        return remote(source, piece, wx_s.at[lo, way], wx_r.at[lo, way], x_prev if way % 2 else x_next)

    def wy(lo, step, way):
        piece = wbuf.at[block(lo, step), pl.ds(mine + way * QUARTER, QUARTER)]
        at = step * 2 + way
        return remote(piece, piece, wy_s.at[lo, at], wy_r.at[lo, at], y_next if way else y_prev)

    def wc(lo, step, src=None):
        piece = wbuf.at[block(lo, step)]
        return remote(piece if src is None else src, piece, wc_s.at[lo, step], wc_r.at[lo, step], partner)

    keep = pltpu.make_async_copy(w_ref, wbuf.at[lat], own_sem)
    keep.start()
    own_half, there = w_ref.at[pl.ds(mine, HALF)], wbuf.at[lat, pl.ds(mine, HALF)]
    go(remote(own_half, there, wz_s.at[0], wz_r.at[0], z_next))
    go(remote(own_half, there, wz_s.at[1], wz_r.at[1], z_prev))
    for copy in (wx(low, 0, w_ref), wx(low, 1, w_ref), wc(low, 0, w_ref)):
        copy.start()
    for lo in range(3):
        sent.extend((wx(lo, 0), wx(lo, 1), wc(lo, 0)))

    def spread(lo):
        @pl.when(low != lo)
        def _():
            side = 2 - mod(lo - low + 3, 3)
            here = wbuf.at[block(lo, 0), pl.ds(mine, HALF)]
            remote(own_half, here, wz_s.at[0], wz_r.at[side], z_next).wait_recv()
            for copy in (wx(lo, 0), wx(lo, 1), wy(lo, 0, 0), wy(lo, 0, 1)):
                copy.start()

    def pass_on(lo):
        for way in range(2):
            wx(lo, way).wait_recv()
            go(wx(lo, 2 + way))
            go(wy(lo, 1 + way, 0))
            go(wy(lo, 1 + way, 1))

    def relay(lo):
        wx(lo, 2).wait_recv()
        wx(lo, 3).wait_recv()
        go(wy(lo, 3, 0))
        go(wy(lo, 3, 1))

    def finish(lo):
        @pl.when(low != lo)
        def _():
            wy(lo, 0, 0).wait_recv()
            wy(lo, 0, 1).wait_recv()
            wc(lo, 0).start()

        for step in range(1, 4):
            wy(lo, step, 0).wait_recv()
            wy(lo, step, 1).wait_recv()
            go(wc(lo, step))

    def arrived(lo):
        for step in range(4):
            wc(lo, step).wait_recv()

    gain = gain_conv[...]

    def norm_row(row, carry):
        value = f_ref[row].astype(F32)
        mean = jnp.mean(value * value, axis=-1, keepdims=True)
        value = (value * lax.rsqrt(mean + EPS) * gain).astype(BF)
        normed[row] = value
        wide = value.astype(F32)
        for k in range(8):
            pad[k, row + REACH, REACH : REACH + 16, :] = wide[:, k * 128 : (k + 1) * 128]
        return carry

    lax.fori_loop(0, 16, norm_row, 0)

    down = remote(normed.at[pl.ds(13, 3)], lat_in.at[0], lat_s.at[0], lat_r.at[0], lat_next)
    up = remote(normed.at[pl.ds(0, 3)], lat_in.at[1], lat_s.at[1], lat_r.at[1], lat_prev)

    @pl.when(lat < 23)
    def _():
        down.start()

    @pl.when(lat > 0)
    def _():
        up.start()

    sides = ((0, 16, lon_next), (1, REACH, lon_prev))
    lon_copies, corner_copies = [], []
    for side, first, device in sides:
        for row in range(16):
            for k in range(8):
                strip32[pl.ds(row * 3, 3), k * 128 : (k + 1) * 128] = pad[k, row + REACH, first : first + 3, :]
        strip16[side] = strip32[...].astype(BF)
        lon_copies.append(go(remote(strip16.at[side], lon_in.at[side], lon_s.at[side], lon_r.at[side], device)))

    for side, here, base in ((0, lat > 0, 0), (1, lat < 23, 19)):
        copy = down if side == 0 else up

        @pl.when(here)
        def _():
            copy.wait_recv()
            for row in range(3):
                wide = lat_in[side, row].astype(F32)
                for k in range(8):
                    pad[k, base + row, REACH : REACH + 16, :] = wide[:, k * 128 : (k + 1) * 128]

        @pl.when(jnp.logical_not(here))
        def _():
            for row in range(3):
                for k in range(8):
                    pad[k, base + row, REACH : REACH + 16, :] = jnp.zeros((16, 128), F32)

    strip32[pl.ds(16, 8), :] = jnp.zeros((8, C), F32)
    for side, first, device in sides:
        for n in range(6):
            row = n if n < 3 else n + 16
            for k in range(8):
                strip32[pl.ds(n * 3, 3), k * 128 : (k + 1) * 128] = pad[k, row, first : first + 3, :]
        corner_out[side] = strip32[pl.ds(0, 24), :].astype(BF)
        corner_copies.append(
            go(remote(corner_out.at[side], corner_in.at[side], corner_s.at[side], corner_r.at[side], device))
        )

    deep = 8

    def depthwise(top):
        def lanes(k, carry):
            at = pl.multiple_of(k * 128, 128)
            total = [None] * deep
            for b in range(KERNEL):
                for row in range(deep + 2 * REACH):
                    value = pad[k, top + row, b : b + 16, :]
                    for a in range(KERNEL):
                        i = row - a
                        if 0 <= i < deep:
                            term = value * w_depth[a, b : b + 1, pl.ds(at, 128)]
                            total[i] = term if total[i] is None else total[i] + term
            for i in range(deep):
                inner[k, top + i] = total[i]
            return carry

        lax.fori_loop(0, 8, lanes, 0)

    def neighbours(top):
        def lanes(k, carry):
            at = pl.multiple_of(k * 128, 128)
            total = [[inner[k, top + i, side * 8 : side * 8 + 8, :] for i in range(deep)] for side in range(2)]
            for side in range(2):
                for shift in range(REACH):
                    b = shift + 4 * side
                    for row in range(deep + 2 * REACH):
                        value = edge[side, k, top + row, shift : shift + 8, :]
                        for a in range(KERNEL):
                            i = row - a
                            if 0 <= i < deep:
                                total[side][i] += value * w_depth[a, b : b + 1, pl.ds(at, 128)]
            for i in range(deep):
                both = jnp.concatenate([total[0][i], total[1][i]], axis=0)
                conv[pl.ds((top + i) * 16, 16), pl.ds(at, 128)] = both.astype(BF)
            return carry

        lax.fori_loop(0, 8, lanes, 0)

    def weights(n):
        return jnp.concatenate([wbuf[2 * n], wbuf[2 * n + 1]], axis=1)

    def pointwise(start):
        rows = pl.ds(start, MIX_ROWS)
        value = conv[rows, :]

        def columns(n, carry):
            at = pl.ds(pl.multiple_of(n * 256, 256), 256)
            own = f_ref[pl.ds(start // 16, MIX_ROWS // 16), :, at].reshape(MIX_ROWS, 256)
            mixed[rows, at] = own.astype(F32) + jnp.dot(value, weights(n), preferred_element_type=F32)
            return carry

        lax.fori_loop(0, 4, columns, 0)

    attn_gain = gain_attn[...]

    def attn_norm(start):
        def some(n, carry):
            rows = pl.ds(pl.multiple_of(start + n * 32, 32), 32)
            value = mixed[rows, :]
            mean = jnp.mean(value * value, axis=-1, keepdims=True)
            moved_out[rows, :] = (value * lax.rsqrt(mean + EPS) * attn_gain).astype(BF)
            return carry

        lax.fori_loop(0, IN_ROWS // 32, some, 0)

    spread(0)
    spread(2)
    pass_on(0)
    depthwise(0)
    relay(0)
    spread(1)
    depthwise(deep)
    finish(0)
    keep.wait()
    for side, first in ((0, 0), (1, 7)):
        lon_copies[side].wait_recv()
        strip32[...] = lon_in[side].astype(F32)
        for row in range(16):
            for k in range(8):
                edge[side, k, row + REACH, first : first + 3, :] = strip32[pl.ds(row * 3, 3), k * 128 : (k + 1) * 128]
    for side, first in ((0, 0), (1, 7)):
        corner_copies[side].wait_recv()
        strip32[pl.ds(0, 24), :] = corner_in[side].astype(F32)
        for n in range(6):
            row = n if n < 3 else n + 16
            for k in range(8):
                edge[side, k, row, first : first + 3, :] = strip32[pl.ds(n * 3, 3), k * 128 : (k + 1) * 128]
    neighbours(0)
    pass_on(2)
    neighbours(deep)
    arrived(0)
    moves = []
    for i in range(256 // MIX_ROWS):
        pointwise(i * MIX_ROWS)
        for j in range(i * MIX_ROWS // IN_ROWS, (i + 1) * MIX_ROWS // IN_ROWS):
            attn_norm(j * IN_ROWS)
            rows = pl.ds(j * IN_ROWS, IN_ROWS)
            moves.append(go(remote(moved_out.at[rows], moved_in.at[rows], in_s.at[j], in_r.at[j], target)))

    relay(2)
    finish(2)
    pass_on(1)
    relay(1)
    arrived(2)

    pieces = []
    for i in range(256 // IN_ROWS):
        rows = pl.ds(i * IN_ROWS, IN_ROWS)
        moves[i].wait_recv()
        value = moved_in[rows, :]

        def columns(n, carry):
            at = pl.ds(pl.multiple_of(n * 256, 256), 256)
            kv[0, rows, at] = jnp.dot(value, weights(n + 8), preferred_element_type=F32).astype(BF)
            return carry

        lax.fori_loop(0, 4, columns, 0)
        pieces.append(
            [
                go(remote(kv.at[0, rows], kv.at[to, rows], kv_s.at[i, to], kv_r.at[i, to], device))
                for to, device in ((3, near), (2, far), (1, partner))
            ]
        )

    finish(1)
    arrived(1)

    left_half = lax.broadcasted_iota(jnp.int32, (256, 128), 1) < 64

    def queries(i, carry):
        value = jnp.dot(moved_in[...], weights(i + 4), preferred_element_type=F32)
        value = value.astype(BF).astype(F32) * 0.125
        first, second = value[:, :128], value[:, 128:]
        zero = jnp.zeros_like(first)
        qz[i, 0] = jnp.where(left_half, first, zero).astype(BF)
        qz[i, 1] = jnp.where(left_half, pltpu.roll(first, 64, 1), zero).astype(BF)
        qz[i, 2] = jnp.where(left_half, zero, pltpu.roll(second, 64, 1)).astype(BF)
        qz[i, 3] = jnp.where(left_half, zero, second).astype(BF)
        return carry

    lax.fori_loop(0, 4, queries, 0)

    for i, (to_near, to_far, to_partner) in enumerate(pieces):
        rows = pl.ds(i * IN_ROWS, IN_ROWS)
        to_near.wait_recv()
        to_near = go(remote(kv.at[3, rows], kv.at[4, rows], kv_s.at[i, 4], kv_r.at[i, 4], partner))
        pieces[i].append(to_near)
    for _, to_far, to_partner, relayed in pieces:
        to_far.wait_recv()
        to_partner.wait_recv()
        relayed.wait_recv()

    out_gain = gain_out[...]
    def attend(start, size):
        rows = pl.ds(start, size)
        half = lax.broadcasted_iota(jnp.int32, (size, 128), 1) < 64

        def heads(i, carry):
            at = pl.ds(pl.multiple_of(i * 128, 128), 128)
            values_at = pl.ds(pl.multiple_of(i * 128 + C // 2, 128), 128)
            query = qz[i, :, rows, :].reshape(4 * size, 128)
            keys = kv[:, :, at].reshape(1280, 128)
            values = kv[:, :, values_at].reshape(1280, 128)
            scores = lax.dot_general(query, keys, (((1,), (1,)), ((), ())), preferred_element_type=F32)
            peak = jnp.max(scores, axis=-1, keepdims=True)
            expo = jnp.exp(scores - peak).astype(BF)
            wide = jnp.concatenate([values, jnp.ones((1280, 128), BF)], axis=1)
            both = jnp.dot(expo, wide, preferred_element_type=F32)
            result = (both[:, :128] / both[:, 128:]).reshape(4, size, 128)
            first = jnp.where(half, result[0], pltpu.roll(result[1], 64, 1))
            second = jnp.where(half, pltpu.roll(result[2], 64, 1), result[3])
            out_at = pl.multiple_of(i * 256, 256)
            attended[pl.ds(0, size), pl.ds(out_at, 128)] = first
            attended[pl.ds(0, size), pl.ds(out_at + 128, 128)] = second
            return carry

        lax.fori_loop(0, 4, heads, 0)
        value = attended[pl.ds(0, size), :]
        mean = jnp.mean(value * value, axis=-1, keepdims=True)
        back_out[rows, :] = (value * lax.rsqrt(mean + EPS) * out_gain).astype(BF)

    backs, start = [], 0
    for i, size in enumerate(OUT_ROWS):
        attend(start, size)
        rows = pl.ds(start, size)
        backs.append(go(remote(back_out.at[rows], back_in.at[rows], back_s.at[i], back_r.at[i], origin)))
        start += size
    for copy in backs:
        copy.wait_recv()

    for copy in sent:
        copy.wait_send()
    for lo in range(3):

        @pl.when(low != lo)
        def _():
            wy(lo, 0, 0).wait_send()
            wy(lo, 0, 1).wait_send()

    @pl.when(lat < 23)
    def _():
        down.wait_send()

    @pl.when(lat > 0)
    def _():
        up.wait_send()


def per_device(fields, gain_conv, w_depth, w_layer, gain_attn, gain_out):
    vmem = pl.BlockSpec(memory_space=pltpu.VMEM)
    dma = pltpu.SemaphoreType.DMA
    n_in, n_out = 256 // IN_ROWS, len(OUT_ROWS)
    mixed, back = pl.pallas_call(
        kernel,
        out_shape=[jax.ShapeDtypeStruct((256, C), F32), jax.ShapeDtypeStruct((256, C), BF)],
        in_specs=[vmem, vmem, vmem, pl.BlockSpec(memory_space=pl.ANY), vmem, vmem],
        out_specs=[vmem, vmem],
        scratch_shapes=[
            pltpu.VMEM((24, C, 128), BF),
            pltpu.VMEM((8, 22, 24, 128), F32),
            pltpu.VMEM((2, 8, 22, 16, 128), F32),
            pltpu.VMEM((8, 16, 16, 128), F32),
            pltpu.VMEM((16, 16, C), BF),
            pltpu.VMEM((2, 3, 16, C), BF),
            pltpu.VMEM((48, C), F32),
            pltpu.VMEM((2, 48, C), BF),
            pltpu.VMEM((2, 48, C), BF),
            pltpu.VMEM((2, 24, C), BF),
            pltpu.VMEM((2, 24, C), BF),
            pltpu.VMEM((256, C), BF),
            pltpu.VMEM((256, C), BF),
            pltpu.VMEM((256, C), BF),
            pltpu.VMEM((4, 4, 256, 128), BF),
            pltpu.VMEM((5, 256, C), BF),
            pltpu.VMEM((max(OUT_ROWS), C), F32),
            pltpu.VMEM((256, C), BF),
            dma,
            dma((2,)), dma((2,)),
            dma((3, 4)), dma((3, 4)),
            dma((3, 8)), dma((3, 8)),
            dma((3, 4)), dma((3, 4)),
            dma((2,)), dma((2,)),
            dma((2,)), dma((2,)),
            dma((2,)), dma((2,)),
            dma((n_in,)), dma((n_in,)),
            dma((n_in, 5)), dma((n_in, 5)),
            dma((n_out,)), dma((n_out,)),
        ],
        compiler_params=pltpu.CompilerParams(
            collective_id=0, has_side_effects=True, vmem_limit_bytes=60 * 1024 * 1024
        ),
        name="layer",
    )(
        fields, gain_conv.reshape(1, C), w_depth, w_layer,
        gain_attn.reshape(1, C), gain_out.reshape(1, C),
    )
    return (mixed + back.astype(F32)).astype(BF).reshape(fields.shape)


def solution(mesh):
    return jax.shard_map(
        per_device,
        mesh=mesh,
        in_specs=(P("lat", "lon", None), P(), P(), P(None, "lat"), P(), P()),
        out_specs=P("lat", "lon", None),
        check_vma=False,
    )
```

```python
import functools

import jax
import jax.numpy as jnp
from jax import lax
from jax.experimental import pallas as pl
from jax.experimental.pallas import tpu as pltpu
from jax.sharding import PartitionSpec as P

C = 1024
KERNEL = 7
REACH = 3
EPS = 1e-06
MIX_ROWS = 128
IN_ROWS = 64
OUT_ROWS = (32, 32, 64, 64, 64)
BF = jnp.bfloat16
F32 = jnp.float32


def div(a, b):
    return lax.div(a, jnp.int32(b))


def mod(a, b):
    return lax.rem(a, jnp.int32(b))


def home_device(x, y, z, core):
    return (mod(z, 3) * 4 + x) * 2 + core, y * 4 + div(z, 3)


BAND_Z = (10, 7, 11, 5, 8, 2, 3, 9, 1, 4, 6, 0)
BAND_FLIP = (0, 0, 1, 1, 1, 0, 0, 0, 1, 1, 0, 0)


def pick(table, index):
    value = jnp.int32(0)
    for i, entry in enumerate(table):
        if entry:
            value = value + jnp.where(index == i, jnp.int32(entry), jnp.int32(0))
    return value


def work_device(band, x_pair, sector):
    y, high = div(sector, 4), mod(sector, 4)
    x = 2 * x_pair + mod(div(high, 2) + y + pick(BAND_FLIP, band), 2)
    return home_device(x, y, pick(BAND_Z, band), mod(high, 2))


def remote(src, dst, sends, recvs, device):
    return pltpu.make_async_remote_copy(
        src_ref=src,
        dst_ref=dst,
        send_sem=sends,
        recv_sem=recvs,
        device_id=device,
        device_id_type=pl.DeviceIdType.MESH,
    )


def kernel(
    f_ref, gain_conv, w_depth, w_ref, gain_attn, gain_out, mixed, back_in,
    wbuf, pad, edge, inner, normed, lat_in, strip32, strip16, lon_in, corner_out, corner_in, conv, moved_out, moved_in,
    qz, kv, attended, back_out,
    own_sem, wz_s, wz_r, wx_s, wx_r, wy_s, wy_r, wc_s, wc_r, lat_s, lat_r, lon_s, lon_r, corner_s, corner_r,
    in_s, in_r, kv_s, kv_r, back_s, back_r,
):
    lat, lon = lax.axis_index("lat"), lax.axis_index("lon")
    core, x, low = mod(lat, 2), mod(div(lat, 2), 4), div(lat, 8)
    y, high = div(lon, 4), mod(lon, 4)
    z = high * 3 + low
    z_next = home_device(x, y, mod(z + 1, 12), core)
    z_prev = home_device(x, y, mod(z + 11, 12), core)
    x_next = ((low * 4 + mod(x + 1, 4)) * 2 + core, lon)
    x_prev = ((low * 4 + mod(x + 3, 4)) * 2 + core, lon)
    partner = (lat + 1 - 2 * core, lon)
    lat_next, lat_prev = (mod(lat + 1, 24), lon), (mod(lat + 23, 24), lon)
    lon_next, lon_prev = (lat, mod(lon + 1, 32)), (lat, mod(lon + 31, 32))
    y_next, y_prev = (lat, mod(lon + 4, 32)), (lat, mod(lon + 28, 32))
    x_pair = div(x, 2)
    band = pick([BAND_Z.index(i) for i in range(12)], z)
    part = mod(mod(x, 2) + y + pick(BAND_FLIP, band), 2)
    sector = y * 4 + 2 * part + core
    origin = ((div(band, 4) * 4 + 2 * x_pair + mod(div(band, 2), 2)) * 2 + mod(band, 2), sector)
    target = work_device(low * 4 + mod(x, 2) * 2 + core, x_pair, lon)
    outward = 1 - 2 * core
    near = work_device(band, x_pair, mod(sector - outward + 32, 32))
    far = work_device(band, x_pair, mod(sector + 2 * outward + 32, 32))
    far_from = work_device(band, x_pair, mod(sector - 2 * outward + 32, 32))

    barrier = pltpu.get_barrier_semaphore()
    greeted = (
        z_next, z_prev, x_next, x_prev, y_next, y_prev, partner, lat_next, lat_prev, lon_next, lon_prev,
        origin, target, near, far_from,
    )
    for device in greeted:
        pl.semaphore_signal(
            barrier, inc=1, device_id=device, device_id_type=pl.DeviceIdType.MESH
        )

    def clear(row, carry):
        zero = jnp.zeros((8, 128), F32)
        for k in range(8):
            for first in (0, 16):
                pad[k, row, first : first + 8, :] = zero
            for side in range(2):
                for first in (0, 8):
                    edge[side, k, row, first : first + 8, :] = zero
        return carry

    lax.fori_loop(0, 22, clear, 0)
    pl.semaphore_wait(barrier, len(greeted))

    sent = []

    def go(copy):
        copy.start()
        sent.append(copy)
        return copy

    HALF, QUARTER = C // 2, C // 4
    mine = pl.multiple_of(mod(y, 2) * HALF, HALF)

    def block(lo, step):
        return (lo * 4 + mod(x + (0, 3, 1, 2)[step], 4)) * 2 + core

    def wx(lo, way, src=None):
        b = block(lo, (0, 0, 1, 2)[way])
        rows = (pl.ds(mine, HALF), pl.ds(mine, HALF), pl.ds(mine, QUARTER), pl.ds(mine + QUARTER, QUARTER))[way]
        piece = wbuf.at[b, rows]
        source = piece if src is None else src.at[rows]
        return remote(source, piece, wx_s.at[lo, way], wx_r.at[lo, way], x_prev if way % 2 else x_next)

    def wy(lo, step, way):
        piece = wbuf.at[block(lo, step), pl.ds(mine + way * QUARTER, QUARTER)]
        at = step * 2 + way
        return remote(piece, piece, wy_s.at[lo, at], wy_r.at[lo, at], y_next if way else y_prev)

    def wc(lo, step, src=None):
        piece = wbuf.at[block(lo, step)]
        return remote(piece if src is None else src, piece, wc_s.at[lo, step], wc_r.at[lo, step], partner)

    keep = pltpu.make_async_copy(w_ref, wbuf.at[lat], own_sem)
    keep.start()
    own_half, there = w_ref.at[pl.ds(mine, HALF)], wbuf.at[lat, pl.ds(mine, HALF)]
    go(remote(own_half, there, wz_s.at[0], wz_r.at[0], z_next))
    go(remote(own_half, there, wz_s.at[1], wz_r.at[1], z_prev))
    for copy in (wx(low, 0, w_ref), wx(low, 1, w_ref), wc(low, 0, w_ref)):
        copy.start()
    for lo in range(3):
        sent.extend((wx(lo, 0), wx(lo, 1), wc(lo, 0)))

    def spread(lo):
        @pl.when(low != lo)
        def _():
            side = 2 - mod(lo - low + 3, 3)
            here = wbuf.at[block(lo, 0), pl.ds(mine, HALF)]
            remote(own_half, here, wz_s.at[0], wz_r.at[side], z_next).wait_recv()
            for copy in (wx(lo, 0), wx(lo, 1), wy(lo, 0, 0), wy(lo, 0, 1)):
                copy.start()

    def pass_on(lo):
        for way in range(2):
            wx(lo, way).wait_recv()
            go(wx(lo, 2 + way))
            go(wy(lo, 1 + way, 0))
            go(wy(lo, 1 + way, 1))

    def relay(lo):
        wx(lo, 2).wait_recv()
        wx(lo, 3).wait_recv()
        go(wy(lo, 3, 0))
        go(wy(lo, 3, 1))

    def finish(lo):
        @pl.when(low != lo)
        def _():
            wy(lo, 0, 0).wait_recv()
            wy(lo, 0, 1).wait_recv()
            wc(lo, 0).start()

        for step in range(1, 4):
            wy(lo, step, 0).wait_recv()
            wy(lo, step, 1).wait_recv()
            go(wc(lo, step))

    def arrived(lo):
        for step in range(4):
            wc(lo, step).wait_recv()

    gain = gain_conv[...]

    def norm_row(row, carry):
        value = f_ref[row].astype(F32)
        mean = jnp.mean(value * value, axis=-1, keepdims=True)
        value = (value * lax.rsqrt(mean + EPS) * gain).astype(BF)
        normed[row] = value
        wide = value.astype(F32)
        for k in range(8):
            pad[k, row + REACH, REACH : REACH + 16, :] = wide[:, k * 128 : (k + 1) * 128]
        return carry

    lax.fori_loop(0, 16, norm_row, 0)

    down = remote(normed.at[pl.ds(13, 3)], lat_in.at[0], lat_s.at[0], lat_r.at[0], lat_next)
    up = remote(normed.at[pl.ds(0, 3)], lat_in.at[1], lat_s.at[1], lat_r.at[1], lat_prev)

    @pl.when(lat < 23)
    def _():
        down.start()

    @pl.when(lat > 0)
    def _():
        up.start()

    sides = ((0, 16, lon_next), (1, REACH, lon_prev))
    lon_copies, corner_copies = [], []
    for side, first, device in sides:
        for row in range(16):
            for k in range(8):
                strip32[pl.ds(row * 3, 3), k * 128 : (k + 1) * 128] = pad[k, row + REACH, first : first + 3, :]
        strip16[side] = strip32[...].astype(BF)
        lon_copies.append(go(remote(strip16.at[side], lon_in.at[side], lon_s.at[side], lon_r.at[side], device)))

    for side, here, base in ((0, lat > 0, 0), (1, lat < 23, 19)):
        copy = down if side == 0 else up

        @pl.when(here)
        def _():
            copy.wait_recv()
            for row in range(3):
                wide = lat_in[side, row].astype(F32)
                for k in range(8):
                    pad[k, base + row, REACH : REACH + 16, :] = wide[:, k * 128 : (k + 1) * 128]

        @pl.when(jnp.logical_not(here))
        def _():
            for row in range(3):
                for k in range(8):
                    pad[k, base + row, REACH : REACH + 16, :] = jnp.zeros((16, 128), F32)

    strip32[pl.ds(16, 8), :] = jnp.zeros((8, C), F32)
    for side, first, device in sides:
        for n in range(6):
            row = n if n < 3 else n + 16
            for k in range(8):
                strip32[pl.ds(n * 3, 3), k * 128 : (k + 1) * 128] = pad[k, row, first : first + 3, :]
        corner_out[side] = strip32[pl.ds(0, 24), :].astype(BF)
        corner_copies.append(
            go(remote(corner_out.at[side], corner_in.at[side], corner_s.at[side], corner_r.at[side], device))
        )

    deep = 8

    def depthwise(top):
        def lanes(k, carry):
            at = pl.multiple_of(k * 128, 128)
            total = [None] * deep
            for b in range(KERNEL):
                for row in range(deep + 2 * REACH):
                    value = pad[k, top + row, b : b + 16, :]
                    for a in range(KERNEL):
                        i = row - a
                        if 0 <= i < deep:
                            term = value * w_depth[a, b : b + 1, pl.ds(at, 128)]
                            total[i] = term if total[i] is None else total[i] + term
            for i in range(deep):
                inner[k, top + i] = total[i]
            return carry

        lax.fori_loop(0, 8, lanes, 0)

    def neighbours(top):
        def lanes(k, carry):
            at = pl.multiple_of(k * 128, 128)
            total = [[inner[k, top + i, side * 8 : side * 8 + 8, :] for i in range(deep)] for side in range(2)]
            for side in range(2):
                for shift in range(REACH):
                    b = shift + 4 * side
                    for row in range(deep + 2 * REACH):
                        value = edge[side, k, top + row, shift : shift + 8, :]
                        for a in range(KERNEL):
                            i = row - a
                            if 0 <= i < deep:
                                total[side][i] += value * w_depth[a, b : b + 1, pl.ds(at, 128)]
            for i in range(deep):
                both = jnp.concatenate([total[0][i], total[1][i]], axis=0)
                conv[pl.ds((top + i) * 16, 16), pl.ds(at, 128)] = both.astype(BF)
            return carry

        lax.fori_loop(0, 8, lanes, 0)

    def weights(n):
        return jnp.concatenate([wbuf[2 * n], wbuf[2 * n + 1]], axis=1)

    def pointwise(start):
        rows = pl.ds(start, MIX_ROWS)
        value = conv[rows, :]

        def columns(n, carry):
            at = pl.ds(pl.multiple_of(n * 256, 256), 256)
            own = f_ref[pl.ds(start // 16, MIX_ROWS // 16), :, at].reshape(MIX_ROWS, 256)
            mixed[rows, at] = own.astype(F32) + jnp.dot(value, weights(n), preferred_element_type=F32)
            return carry

        lax.fori_loop(0, 4, columns, 0)

    attn_gain = gain_attn[...]

    def attn_norm(start):
        def some(n, carry):
            rows = pl.ds(pl.multiple_of(start + n * 32, 32), 32)
            value = mixed[rows, :]
            mean = jnp.mean(value * value, axis=-1, keepdims=True)
            moved_out[rows, :] = (value * lax.rsqrt(mean + EPS) * attn_gain).astype(BF)
            return carry

        lax.fori_loop(0, IN_ROWS // 32, some, 0)

    spread(0)
    spread(2)
    pass_on(0)
    depthwise(0)
    relay(0)
    spread(1)
    depthwise(deep)
    finish(0)
    keep.wait()
    for side, first in ((0, 0), (1, 7)):
        lon_copies[side].wait_recv()
        strip32[...] = lon_in[side].astype(F32)
        for row in range(16):
            for k in range(8):
                edge[side, k, row + REACH, first : first + 3, :] = strip32[pl.ds(row * 3, 3), k * 128 : (k + 1) * 128]
    for side, first in ((0, 0), (1, 7)):
        corner_copies[side].wait_recv()
        strip32[pl.ds(0, 24), :] = corner_in[side].astype(F32)
        for n in range(6):
            row = n if n < 3 else n + 16
            for k in range(8):
                edge[side, k, row, first : first + 3, :] = strip32[pl.ds(n * 3, 3), k * 128 : (k + 1) * 128]
    neighbours(0)
    pass_on(2)
    neighbours(deep)
    arrived(0)
    moves = []
    for i in range(256 // MIX_ROWS):
        pointwise(i * MIX_ROWS)
        for j in range(i * MIX_ROWS // IN_ROWS, (i + 1) * MIX_ROWS // IN_ROWS):
            attn_norm(j * IN_ROWS)
            rows = pl.ds(j * IN_ROWS, IN_ROWS)
            moves.append(go(remote(moved_out.at[rows], moved_in.at[rows], in_s.at[j], in_r.at[j], target)))

    relay(2)
    finish(2)
    pass_on(1)
    relay(1)
    arrived(2)

    pieces = []
    for i in range(256 // IN_ROWS):
        rows = pl.ds(i * IN_ROWS, IN_ROWS)
        moves[i].wait_recv()
        value = moved_in[rows, :]

        def columns(n, carry):
            at = pl.ds(pl.multiple_of(n * 256, 256), 256)
            kv[0, rows, at] = jnp.dot(value, weights(n + 8), preferred_element_type=F32).astype(BF)
            return carry

        lax.fori_loop(0, 4, columns, 0)
        pieces.append(
            [
                go(remote(kv.at[0, rows], kv.at[to, rows], kv_s.at[i, to], kv_r.at[i, to], device))
                for to, device in ((3, near), (2, far), (1, partner))
            ]
        )

    def hand_over(i):
        rows = pl.ds(i * IN_ROWS, IN_ROWS)
        pieces[i][0].wait_recv()
        pieces[i].append(go(remote(kv.at[3, rows], kv.at[4, rows], kv_s.at[i, 4], kv_r.at[i, 4], partner)))

    for i in range(len(pieces) - 1):
        hand_over(i)

    finish(1)
    arrived(1)

    left_half = lax.broadcasted_iota(jnp.int32, (256, 128), 1) < 64

    def queries(i, carry):
        value = jnp.dot(moved_in[...], weights(i + 4), preferred_element_type=F32)
        value = value.astype(BF).astype(F32) * 0.125
        first, second = value[:, :128], value[:, 128:]
        zero = jnp.zeros_like(first)
        qz[i, 0] = jnp.where(left_half, first, zero).astype(BF)
        qz[i, 1] = jnp.where(left_half, pltpu.roll(first, 64, 1), zero).astype(BF)
        qz[i, 2] = jnp.where(left_half, zero, pltpu.roll(second, 64, 1)).astype(BF)
        qz[i, 3] = jnp.where(left_half, zero, second).astype(BF)
        return carry

    lax.fori_loop(0, 4, queries, 0)

    hand_over(len(pieces) - 1)
    for _, to_far, to_partner, relayed in pieces:
        to_far.wait_recv()
        to_partner.wait_recv()
        relayed.wait_recv()

    out_gain = gain_out[...]
    def attend(start, size):
        rows = pl.ds(start, size)
        half = lax.broadcasted_iota(jnp.int32, (size, 128), 1) < 64

        def heads(i, carry):
            at = pl.ds(pl.multiple_of(i * 128, 128), 128)
            values_at = pl.ds(pl.multiple_of(i * 128 + C // 2, 128), 128)
            query = qz[i, :, rows, :].reshape(4 * size, 128)
            keys = kv[:, :, at].reshape(1280, 128)
            values = kv[:, :, values_at].reshape(1280, 128)
            scores = lax.dot_general(query, keys, (((1,), (1,)), ((), ())), preferred_element_type=F32)
            peak = jnp.max(scores, axis=-1, keepdims=True)
            expo = jnp.exp(scores - peak).astype(BF)
            wide = jnp.concatenate([values, jnp.ones((1280, 128), BF)], axis=1)
            both = jnp.dot(expo, wide, preferred_element_type=F32)
            result = (both[:, :128] / both[:, 128:]).reshape(4, size, 128)
            first = jnp.where(half, result[0], pltpu.roll(result[1], 64, 1))
            second = jnp.where(half, pltpu.roll(result[2], 64, 1), result[3])
            out_at = pl.multiple_of(i * 256, 256)
            attended[pl.ds(0, size), pl.ds(out_at, 128)] = first
            attended[pl.ds(0, size), pl.ds(out_at + 128, 128)] = second
            return carry

        lax.fori_loop(0, 4, heads, 0)
        value = attended[pl.ds(0, size), :]
        mean = jnp.mean(value * value, axis=-1, keepdims=True)
        back_out[rows, :] = (value * lax.rsqrt(mean + EPS) * out_gain).astype(BF)

    backs, start = [], 0
    for i, size in enumerate(OUT_ROWS):
        attend(start, size)
        rows = pl.ds(start, size)
        backs.append(go(remote(back_out.at[rows], back_in.at[rows], back_s.at[i], back_r.at[i], origin)))
        start += size
    for copy in backs:
        copy.wait_recv()

    for copy in sent:
        copy.wait_send()
    for lo in range(3):

        @pl.when(low != lo)
        def _():
            wy(lo, 0, 0).wait_send()
            wy(lo, 0, 1).wait_send()

    @pl.when(lat < 23)
    def _():
        down.wait_send()

    @pl.when(lat > 0)
    def _():
        up.wait_send()


def per_device(fields, gain_conv, w_depth, w_layer, gain_attn, gain_out):
    vmem = pl.BlockSpec(memory_space=pltpu.VMEM)
    dma = pltpu.SemaphoreType.DMA
    n_in, n_out = 256 // IN_ROWS, len(OUT_ROWS)
    mixed, back = pl.pallas_call(
        kernel,
        out_shape=[jax.ShapeDtypeStruct((256, C), F32), jax.ShapeDtypeStruct((256, C), BF)],
        in_specs=[vmem, vmem, vmem, pl.BlockSpec(memory_space=pl.ANY), vmem, vmem],
        out_specs=[vmem, vmem],
        scratch_shapes=[
            pltpu.VMEM((24, C, 128), BF),
            pltpu.VMEM((8, 22, 24, 128), F32),
            pltpu.VMEM((2, 8, 22, 16, 128), F32),
            pltpu.VMEM((8, 16, 16, 128), F32),
            pltpu.VMEM((16, 16, C), BF),
            pltpu.VMEM((2, 3, 16, C), BF),
            pltpu.VMEM((48, C), F32),
            pltpu.VMEM((2, 48, C), BF),
            pltpu.VMEM((2, 48, C), BF),
            pltpu.VMEM((2, 24, C), BF),
            pltpu.VMEM((2, 24, C), BF),
            pltpu.VMEM((256, C), BF),
            pltpu.VMEM((256, C), BF),
            pltpu.VMEM((256, C), BF),
            pltpu.VMEM((4, 4, 256, 128), BF),
            pltpu.VMEM((5, 256, C), BF),
            pltpu.VMEM((max(OUT_ROWS), C), F32),
            pltpu.VMEM((256, C), BF),
            dma,
            dma((2,)), dma((2,)),
            dma((3, 4)), dma((3, 4)),
            dma((3, 8)), dma((3, 8)),
            dma((3, 4)), dma((3, 4)),
            dma((2,)), dma((2,)),
            dma((2,)), dma((2,)),
            dma((2,)), dma((2,)),
            dma((n_in,)), dma((n_in,)),
            dma((n_in, 5)), dma((n_in, 5)),
            dma((n_out,)), dma((n_out,)),
        ],
        compiler_params=pltpu.CompilerParams(
            collective_id=0, has_side_effects=True, vmem_limit_bytes=60 * 1024 * 1024
        ),
        name="layer",
    )(
        fields, gain_conv.reshape(1, C), w_depth, w_layer,
        gain_attn.reshape(1, C), gain_out.reshape(1, C),
    )
    return (mixed + back.astype(F32)).astype(BF).reshape(fields.shape)


def solution(mesh):
    return jax.shard_map(
        per_device,
        mesh=mesh,
        in_specs=(P("lat", "lon", None), P(), P(), P(None, "lat"), P(), P()),
        out_specs=P("lat", "lon", None),
        check_vma=False,
    )
```
